512 devices in a mesh: cfg: 2 (over x_lo), seq: 256 (over y, x_hi, z, core).
Axes of the slice: x: 4 (x_hi: 2, x_lo: 2; x = x_hi * 2 + x_lo), y: 4, z: 16, core: 2. Of those that a mesh axis runs over, the one named last changes fastest.
Arguments:
- img_queries: bfloat16 [2, 3072, 1216], P('cfg', 'seq')
- img_keys: bfloat16 [2, 3072, 1216], P('cfg', 'seq')
- img_values: bfloat16 [2, 3072, 1216], P('cfg', 'seq'), may hold values from -6 to 6
- text_keys: bfloat16 [2, 256, 1216], P('cfg', 'seq'), may hold values from -6 to 6
- text_values: bfloat16 [2, 256, 1216], P('cfg', 'seq'), may hold values from -18 to 18
- query_gain: float32 [64], replicated, may hold values from 0.5 to 8, as said below
- key_gain: float32 [64], replicated, may hold values from 0.5 to 8, as said below
- text_gain: float32 [64], replicated, may hold values from 0.5 to 8, as said below
- text_lengths: int32 [2], P('cfg'), may hold values from 1 to 256, as said below
- text_blocks: int32 [2, 256], P('cfg', 'seq'), may hold values from 0 to 1
- latent: float32 [3072, 64], P('seq', 'cfg'), may hold values from -6 to 6
- base_velocity: bfloat16 [2, 3072, 64], P('cfg', 'seq'), may hold values from -6 to 6
- out_weight: bfloat16 [1216, 64], replicated, may hold values from -1.25 to 1.25
- timestep: int32 [1], replicated, may hold values from 0 to 27
Outputs:
- next_latent: float32 [3072, 64], P('seq', 'cfg')
- denoised: float32 [3072, 64], P('seq', 'cfg')
The draws below stay inside these ranges and needn't reach their ends.
Inputs may be any that keep to these rules, and one draw needn't show every extreme that they name: `query_gain`: gains are positive. `key_gain`: gains are positive. `text_gain`: gains are positive. `text_lengths`: one of the two halves has all 256 slots within its length.
All inputs are finite; a program needn't handle non-finite values.
Results may differ from the reference program's by a relative error of at most 0.007.
The reference program's roundings to bfloat16 on the way count: a program that leaves them out, or rounds other values in their place, can miss the bound.
Values may be sent and summed in bfloat16 or wider, within the bound.
No kernel may reach another device: no remote copies, remote signals or barrier semaphores. Data moves between devices by JAX's collectives and lax.ppermute only.
A program may use at most 128 MiB of HBM per device.

```python
import math
import jax
import jax.numpy as jnp
from jax import lax

HEADS = 19
D_HEAD = 64
CH = 64
TXT_DEV = 1
STEPS = 28
IMG = 3072
TXT = 256


def pair_tokens(key):
    width = HEADS * D_HEAD
    base_queries = jax.random.normal(jax.random.fold_in(key, 101), (2, IMG, width), jnp.float32)
    base_keys = jax.random.normal(jax.random.fold_in(key, 202), (2, IMG, width), jnp.float32)
    return (base_queries, base_keys)


def draw_img_queries(key, part):
    return pair_tokens(key)[0].astype(jnp.bfloat16)


def draw_img_keys(key, part):
    return pair_tokens(key)[1].astype(jnp.bfloat16)


def gain_vector(key, salt):
    sub_key = jax.random.fold_in(key, salt)
    return jnp.exp(jax.random.uniform(sub_key, (D_HEAD,), jnp.float32, minval=math.log(0.5), maxval=math.log(2.0)))


def draw_query_gain(key, part):
    return gain_vector(key, 11)


def draw_key_gain(key, part):
    return gain_vector(key, 12)


def draw_text_gain(key, part):
    return gain_vector(key, 13)


def draw_text_lengths(key, part):
    drawn = jax.random.randint(jax.random.fold_in(key, 55), (2,), 1, TXT + 1, dtype=jnp.int32)
    full_half = jax.random.randint(jax.random.fold_in(key, 56), (), 0, 2, dtype=jnp.int32)
    halves = jnp.arange(2, dtype=jnp.int32)
    return jnp.where(halves == full_half, jnp.int32(TXT), drawn).astype(jnp.int32)


def draw_text_blocks(key, part):
    levels = jax.random.randint(jax.random.fold_in(key, 66), (2, TXT // TXT_DEV), 0, 4, dtype=jnp.int32)
    return (levels > 0).astype(jnp.int32)


def level_of(rng, shape, split, smallest, top_value):
    level = 1.0
    for dim, blocks in split:
        draws = jax.random.uniform(jax.random.fold_in(jax.random.fold_in(rng, 6), dim), (blocks,), jnp.float32, smallest / len(split), top_value / len(split))
        level = level * jnp.repeat(jnp.exp(draws), shape[dim] // blocks).reshape((-1,) + (1,) * (len(shape) - 1 - dim))
    return level


def bell_draw(stream_key, shape, deviation, limit, pieces=(), kind=jnp.bfloat16):
    loudness = level_of(stream_key, shape, pieces, -0.22, 0.18) if pieces else 1.0
    values = jax.random.normal(stream_key, shape, jnp.float32) * deviation * loudness
    return jnp.minimum(jnp.maximum(values, -limit), limit).astype(kind)


def setup_inputs(seed: int = 0) -> dict:
    arg_keys = jax.random.split(jax.random.key(seed), 15)
    img_queries = draw_img_queries(jax.random.fold_in(arg_keys[14], 71), 0)
    img_keys = draw_img_keys(jax.random.fold_in(arg_keys[14], 71), 0)
    img_values = bell_draw(arg_keys[2], (2, IMG, HEADS * D_HEAD), 1.0, 6.0, ((0, 2), (1, 256)))
    text_keys = bell_draw(arg_keys[3], (2, TXT, HEADS * D_HEAD), 1.0, 6.0, ((0, 2), (1, 256)))
    text_values = bell_draw(arg_keys[4], (2, TXT, HEADS * D_HEAD), 3.0, 18.0, ((0, 2), (1, 256)))
    query_gain = draw_query_gain(jax.random.fold_in(arg_keys[14], 71), 0)
    key_gain = draw_key_gain(jax.random.fold_in(arg_keys[14], 71), 0)
    text_gain = draw_text_gain(jax.random.fold_in(arg_keys[14], 71), 0)
    text_lengths = draw_text_lengths(jax.random.fold_in(arg_keys[14], 71), 0)
    text_blocks = draw_text_blocks(jax.random.fold_in(arg_keys[14], 71), 0)
    latent = bell_draw(arg_keys[10], (IMG, CH), 1.0, 6.0, ((0, 256), (1, 2)), jnp.float32)
    base_velocity = bell_draw(arg_keys[11], (2, IMG, CH), 1.0, 6.0, ((0, 2), (1, 256)))
    out_weight = bell_draw(arg_keys[12], (HEADS * D_HEAD, CH), (HEADS * D_HEAD // 64) ** -0.5, 1.25)
    timestep = jax.random.randint(arg_keys[13], (1,), 0, STEPS).astype(jnp.int32)
    return dict(img_queries=img_queries, img_keys=img_keys, img_values=img_values, text_keys=text_keys, text_values=text_values, query_gain=query_gain, key_gain=key_gain, text_gain=text_gain, text_lengths=text_lengths, text_blocks=text_blocks, latent=latent, base_velocity=base_velocity, out_weight=out_weight, timestep=timestep)


epsilon = 1e-06
guidance = 3.5
shift_factor = 3.0
masked_score = -1e+30

def head_norm(values, gain_row):
    widened = values.astype(jnp.float32).reshape(values.shape[0], -1, gain_row.shape[0])
    scaled = widened * lax.rsqrt(lax.optimization_barrier(jnp.mean(widened * widened, axis=-1, keepdims=True)) + epsilon) * gain_row
    return scaled.astype(jnp.bfloat16)

def sigma_at(position):
    time_left = 1.0 - position / STEPS
    return shift_factor * time_left / (1.0 + (shift_factor - 1.0) * time_left)

def attend_half(queries, keys_image, values_image, keys_text, values_text, usable):
    head_size = queries.shape[2]
    scale = 1.0 / math.sqrt(head_size)
    keys_all = jnp.concatenate([keys_image, keys_text], axis=0)
    values_all = jnp.concatenate([values_image.reshape(values_image.shape[0], -1, head_size), values_text.reshape(values_text.shape[0], -1, head_size)], axis=0)
    valid = jnp.concatenate([jnp.ones((keys_image.shape[0],), dtype=jnp.bool_), usable])

    def one_head(head_input):
        query_head, key_head, value_head = head_input
        scores = jnp.dot(query_head, key_head.T, preferred_element_type=jnp.float32) * scale
        scores = jnp.where(valid[None, :], scores, masked_score)
        row_top = lax.optimization_barrier(jnp.max(scores, axis=-1, keepdims=True))
        exponent = jnp.where(valid[None, :], jnp.exp(scores - row_top), 0.0)
        row_total = lax.optimization_barrier(jnp.sum(exponent, axis=-1))
        summed = jnp.dot(exponent.astype(jnp.bfloat16), value_head, preferred_element_type=jnp.float32)
        return summed / row_total[:, None]
    per_head = lax.map(one_head, (queries.transpose(1, 0, 2), keys_all.transpose(1, 0, 2), values_all.transpose(1, 0, 2)))
    return per_head.transpose(1, 0, 2).reshape(queries.shape[0], -1).astype(jnp.bfloat16)

def reference(img_queries, img_keys, img_values, text_keys, text_values, query_gain, key_gain, text_gain, text_lengths, text_blocks, latent, base_velocity, out_weight, timestep):
    slots = jnp.arange(TXT, dtype=jnp.int32)
    velocities = []
    for guide_half in range(2):
        queries = head_norm(img_queries[guide_half], query_gain)
        keys_image = head_norm(img_keys[guide_half], key_gain)
        keys_text = head_norm(text_keys[guide_half], text_gain)
        block_flag = text_blocks[guide_half][slots // TXT_DEV]
        usable = (slots < text_lengths[guide_half]) & (block_flag == 1)
        attended = attend_half(queries, keys_image, img_values[guide_half], keys_text, text_values[guide_half], usable)
        velocity = base_velocity[guide_half].astype(jnp.float32) + jnp.dot(attended, out_weight, preferred_element_type=jnp.float32)
        velocities.append(velocity)
    guided = velocities[1] + guidance * (velocities[0] - velocities[1])
    step_now = timestep[0].astype(jnp.float32)
    sigma_now = sigma_at(step_now)
    sigma_next = sigma_at(step_now + 1.0)
    next_latent = latent + (sigma_next - sigma_now) * guided
    denoised = latent - sigma_now * guided
    return (next_latent, denoised)
```

```python
import jax
import jax.numpy as jnp
from jax import lax
from jax.experimental import pallas as pl
from jax.experimental.pallas import tpu as pltpu
from jax.sharding import Mesh, PartitionSpec as P

STEPS = 28
HEADS = 19
DH = 64
GROUPS = 4
PER = 5
HALF = 6

epsilon = 1e-06
guidance = 3.5
shift_factor = 3.0
masked_score = -1e30

G = ("zl", "core")
R = ("zh",)
C = ("y", "xh")
SEQ = ("y", "xh", "zh", "zl", "core")

f32 = jnp.float32
bf16 = jnp.bfloat16


def sigma_at(position):
    time_left = 1.0 - position / STEPS
    return shift_factor * time_left / (1.0 + (shift_factor - 1.0) * time_left)


def left_lanes(shape):
    return lax.broadcasted_iota(jnp.int32, shape, len(shape) - 1) < DH


def swap(x):
    return pltpu.roll(x, DH, x.ndim - 1)


def normed(x, gain):
    left = left_lanes(x.shape)
    squares = x * x
    sum_left = jnp.sum(jnp.where(left, squares, 0.0), axis=-1, keepdims=True)
    sum_right = jnp.sum(jnp.where(left, 0.0, squares), axis=-1, keepdims=True)
    root = jnp.where(
        left,
        lax.rsqrt(sum_left / DH + epsilon),
        lax.rsqrt(sum_right / DH + epsilon),
    )
    return (x * root * gain).astype(bf16).astype(f32)


def fold(tile, odd):
    low, high = tile[:HALF], tile[HALF:]
    left = left_lanes(low.shape)
    if odd:
        return jnp.where(left, swap(low), high)
    return jnp.where(left, low, swap(high))


def pack_kernel(copies_q, copies_kv, q, k, v, tk, tv, gains, flag, q_out, kv_out):
    query_gain = gains[0:1]
    key_gain = gains[1:2]
    text_gain = gains[2:3]
    usable = flag[0, 0].astype(f32)
    pairs = (HEADS + 1) // 2
    zero2 = jnp.zeros((2, 128), f32)
    zero1 = jnp.zeros((1, 128), f32)
    left1 = left_lanes((1, 128))
    heads = []
    for p in range(pairs):
        wide = 128 if 128 * (p + 1) <= HEADS * DH else DH
        lanes = slice(128 * p, 128 * p + wide)

        def load(ref):
            x = ref[:, lanes].astype(f32)
            if wide < 128:
                x = jnp.concatenate([x, jnp.zeros((x.shape[0], 128 - wide), f32)], axis=1)
            return x

        qt = normed(load(q), query_gain) * 0.125
        kt = normed(load(k), key_gain)
        vt = load(v)
        tkt = normed(load(tk), text_gain)
        tvt = load(tv)
        for odd in range(2):
            q6 = fold(qt, odd)
            k6 = fold(kt, odd)
            v6 = fold(vt, odd)
            tk1 = swap(tkt) if odd else tkt
            tv1 = swap(tvt) if odd else tvt
            tk1 = jnp.where(left1, tk1, usable)
            tv1 = jnp.where(left1, tv1, 0.0)
            heads.append(
                (
                    jnp.concatenate([q6, zero2], axis=0),
                    jnp.concatenate([k6, tk1, zero1, v6, tv1, zero1], axis=0),
                )
            )
    for g in range(GROUPS):
        own = heads[PER * g : PER * (g + 1)]
        q_msg = jnp.concatenate([h[0] for h in own], axis=0).astype(bf16)
        kv_msg = jnp.concatenate([h[1] for h in own], axis=0).astype(bf16)
        for c in range(copies_q):
            q_out[g * copies_q + c] = q_msg
        for c in range(copies_kv):
            kv_out[g * copies_kv + c] = kv_msg


def rows_of(block):
    return block.reshape(block.shape[0] * block.shape[1], block.shape[2])


def dot_t(a, b):
    return lax.dot_general(a, b, (((1,), (1,)), ((), ())), preferred_element_type=f32)


def attend_kernel(q_in, kv_in, out):
    peers_q = q_in.shape[0]
    peers_k = kv_in.shape[0]
    keys = peers_k * 8
    queries = peers_q * 8
    left_k = left_lanes((keys, 128))
    left_q = left_lanes((queries, 128))
    lane_q = lax.broadcasted_iota(jnp.int32, (queries, 128), 1)
    row_kind = lax.broadcasted_iota(jnp.int32, (1, keys), 1) & 7
    image = row_kind < HALF
    stats = jnp.zeros((queries, 128), f32)
    tiles = []
    for j in range(PER):
        q = rows_of(q_in[:, 8 * j : 8 * j + 8, :].astype(f32))
        kv = kv_in[:, 16 * j : 16 * j + 16, :].astype(f32)
        k = rows_of(kv[:, 0:8])
        v = rows_of(kv[:, 8:16])
        if j == 0:
            pick = (lax.broadcasted_iota(jnp.int32, (8, 128), 1) == DH).astype(bf16)
            flags = dot_t(pick, k.astype(bf16))[0:1]
            text = (row_kind == HALF) & (flags > 0.5)
            bias_l = jnp.where(image | text, 0.0, masked_score)
            bias_r = jnp.where(image, 0.0, masked_score)
        q_same = q.astype(bf16)
        q_swap = swap(q).astype(bf16)
        k_l = jnp.where(left_k, k, 0.0).astype(bf16)
        k_r = jnp.where(left_k, 0.0, k).astype(bf16)
        v_same = v.astype(bf16)
        v_swap = swap(v).astype(bf16)
        sides = []
        for side in range(2):
            s_l = dot_t(q_swap if side else q_same, k_l) + bias_l
            s_r = dot_t(q_same if side else q_swap, k_r) + bias_r
            top = jnp.max(jnp.maximum(s_l, s_r), axis=-1, keepdims=True)
            top = top.astype(bf16).astype(f32)
            p_l = jnp.exp(s_l - top)
            p_r = jnp.exp(s_r - top)
            den = jnp.sum(p_l + p_r, axis=-1, keepdims=True)
            num = jnp.dot(
                p_l.astype(bf16), v_swap if side else v_same, preferred_element_type=f32
            ) + jnp.dot(
                p_r.astype(bf16), v_same if side else v_swap, preferred_element_type=f32
            )
            den_hi = den.astype(bf16).astype(f32)
            lane = 8 * side + j
            stats = jnp.where(lane_q == lane, top, stats)
            stats = jnp.where(lane_q == lane + 16, den_hi, stats)
            stats = jnp.where(lane_q == lane + 32, den - den_hi, stats)
            sides.append(num)
        tiles.append(jnp.where(left_q, sides[0], sides[1]).reshape(peers_q, 8, 128))
    tiles.append(stats.reshape(peers_q, 8, 128))
    for j in range(0, PER + 1, 2):
        pair = jnp.concatenate([tiles[j], tiles[j + 1]], axis=1)
        out[:, 8 * j : 8 * j + 16, :] = pair.astype(bf16)


def merge_kernel(parts_in, weight, out):
    blocks = parts_in.shape[0] // GROUPS
    left = left_lanes((blocks, 8, 128))
    left8 = left_lanes((8, 128))
    total = jnp.zeros((16, DH), f32)
    for g in range(GROUPS):
        part = parts_in[g * blocks : (g + 1) * blocks].astype(f32)
        stats = part[:, 8 * PER :, :]
        den = pltpu.roll(stats, 128 - 16, 2) + pltpu.roll(stats, 128 - 32, 2)
        top = jnp.max(stats, axis=0, keepdims=True)
        scale = jnp.exp(stats - top)
        whole = jnp.sum(scale * den, axis=0, keepdims=True)
        share = scale / whole
        for j in range(PER):
            h = PER * g + j
            if h >= HEADS:
                continue
            each = jnp.where(left, share[:, :, j : j + 1], share[:, :, 8 + j : 9 + j])
            attended = jnp.sum(each * part[:, 8 * j : 8 * j + 8, :], axis=0)
            attended = attended.astype(bf16).astype(f32)
            both = jnp.concatenate(
                [jnp.where(left8, attended, 0.0), jnp.where(left8, 0.0, attended)], axis=0
            ).astype(bf16)
            rows = weight[DH * h : DH * (h + 1), :]
            total += jnp.dot(
                both, jnp.concatenate([rows, rows], axis=0), preferred_element_type=f32
            )
    out[...] = total


def on_device(
    img_queries,
    img_keys,
    img_values,
    text_keys,
    text_values,
    query_gain,
    key_gain,
    text_gain,
    text_lengths,
    text_blocks,
    latent,
    base_velocity,
    out_weight,
    timestep,
):
    count_c = lax.axis_size(C)
    count_r = lax.axis_size(R)
    slot = lax.axis_index(SEQ)
    usable = ((slot < text_lengths[0]) & (text_blocks[0, 0] == 1)).astype(jnp.int32)
    gains = jnp.stack([query_gain, key_gain, text_gain])
    gains = jnp.concatenate([gains, gains], axis=1)
    q_msg, kv_msg = pl.pallas_call(
        lambda *refs: pack_kernel(count_c, count_r, *refs),
        out_shape=(
            jax.ShapeDtypeStruct((GROUPS * count_c, 8 * PER, 128), bf16),
            jax.ShapeDtypeStruct((GROUPS * count_r, 16 * PER, 128), bf16),
        ),
        in_specs=[pl.BlockSpec(memory_space=pltpu.VMEM)] * 6
        + [pl.BlockSpec(memory_space=pltpu.SMEM)],
        name="pack",
    )(
        img_queries[0],
        img_keys[0],
        img_values[0],
        text_keys[0],
        text_values[0],
        gains,
        usable.reshape(1, 1),
    )
    q_got = lax.all_to_all(q_msg, G + C, 0, 0, tiled=True)
    kv_got = lax.all_to_all(kv_msg, G + R, 0, 0, tiled=True)
    parts = pl.pallas_call(
        attend_kernel,
        out_shape=jax.ShapeDtypeStruct((GROUPS * count_c, 8 * PER + 8, 128), bf16),
        name="attend",
    )(q_got, kv_got)
    parts_got = lax.all_to_all(parts, G + C, 0, 0, tiled=True)
    change = pl.pallas_call(
        merge_kernel, out_shape=jax.ShapeDtypeStruct((16, DH), f32), name="merge"
    )(parts_got, out_weight)
    change = jnp.concatenate([change[:HALF], change[8 : 8 + HALF]], axis=0)
    velocity = base_velocity[0].astype(f32) + change
    guide_half = lax.axis_index("cfg")
    width = latent.shape[1]
    own_part = jnp.where(guide_half == 0, velocity[:, :width], velocity[:, width:])
    sent_part = jnp.where(guide_half == 0, velocity[:, width:], velocity[:, :width])
    partner = lax.ppermute(sent_part, "cfg", [(0, 1), (1, 0)])
    cond_part = jnp.where(guide_half == 0, own_part, partner)
    uncond_part = jnp.where(guide_half == 0, partner, own_part)
    guided = uncond_part + guidance * (cond_part - uncond_part)
    step_now = timestep[0].astype(f32)
    sigma_now = sigma_at(step_now)
    sigma_next = sigma_at(step_now + 1.0)
    next_latent = latent + (sigma_next - sigma_now) * guided
    denoised = latent - sigma_now * guided
    return (next_latent, denoised)


def build(fine):
    return jax.shard_map(
        on_device,
        mesh=fine,
        in_specs=(
            P("cfg", SEQ, None),
            P("cfg", SEQ, None),
            P("cfg", SEQ, None),
            P("cfg", SEQ, None),
            P("cfg", SEQ, None),
            P(),
            P(),
            P(),
            P("cfg"),
            P("cfg", SEQ),
            P(SEQ, "cfg"),
            P("cfg", SEQ, None),
            P(),
            P(),
        ),
        out_specs=(P(SEQ, "cfg"), P(SEQ, "cfg")),
        check_vma=False,
    )


def solution(mesh):
    devices = mesh.devices.reshape(2, 4, 2, 8, 2, 2)
    return build(Mesh(devices, ("cfg",) + SEQ))
```

```python
import jax
import jax.numpy as jnp
from jax import lax
from jax.experimental import pallas as pl
from jax.experimental.pallas import tpu as pltpu
from jax.sharding import Mesh, PartitionSpec as P


STEPS = 28
HEADS = 19
DH = 64
GROUPS = 4
PER = 5
HALF = 6

epsilon = 1e-06
guidance = 3.5
shift_factor = 3.0
masked_score = -1e30

G = ("zl", "core")
R = ("zh",)
C = ("y", "xh")
SEQ = ("y", "xh", "zh", "zl", "core")

f32 = jnp.float32
bf16 = jnp.bfloat16


def sigma_at(position):
    time_left = 1.0 - position / STEPS
    return shift_factor * time_left / (1.0 + (shift_factor - 1.0) * time_left)


def left_lanes(shape):
    return lax.broadcasted_iota(jnp.int32, shape, len(shape) - 1) < DH


def swap(x):
    return pltpu.roll(x, DH, x.ndim - 1)


def normed(x, gain):
    left = left_lanes(x.shape)
    squares = x * x
    sum_left = jnp.sum(jnp.where(left, squares, 0.0), axis=-1, keepdims=True)
    sum_right = jnp.sum(jnp.where(left, 0.0, squares), axis=-1, keepdims=True)
    root = jnp.where(
        left,
        lax.rsqrt(sum_left / DH + epsilon),
        lax.rsqrt(sum_right / DH + epsilon),
    )
    return (x * root * gain).astype(bf16).astype(f32)


def fold(tile, odd):
    low, high = tile[:HALF], tile[HALF:]
    left = left_lanes(low.shape)
    if odd:
        return jnp.where(left, swap(low), high)
    return jnp.where(left, low, swap(high))


def head_tiles(refs, gains, wanted):
    for p in range((HEADS + 1) // 2):
        wide = 128 if 128 * (p + 1) <= HEADS * DH else DH
        lanes = slice(128 * p, 128 * p + wide)
        tiles = []
        for ref, gain in zip(refs, gains):
            x = ref[:, lanes].astype(f32)
            if wide < 128:
                x = jnp.concatenate([x, jnp.zeros((x.shape[0], 128 - wide), f32)], axis=1)
            tiles.append(x if gain is None else normed(x, gain))
        for odd in range(2):
            wanted(tiles, odd)


def send_copies(out, copies, heads):
    for g in range(GROUPS):
        message = jnp.concatenate(heads[PER * g : PER * (g + 1)], axis=0).astype(bf16)
        for c in range(copies):
            out[g * copies + c] = message


def pack_keys(copies, k, v, tk, tv, gains, flag, out):
    usable = flag[0, 0].astype(f32)
    zero = jnp.zeros((1, 128), f32)
    left = left_lanes((1, 128))
    heads = []

    def add(tiles, odd):
        kt, vt, tkt, tvt = tiles
        tk1 = swap(tkt) if odd else tkt
        tv1 = swap(tvt) if odd else tvt
        tk1 = jnp.where(left, tk1, usable)
        tv1 = jnp.where(left, tv1, 0.0)
        rows = [fold(kt, odd), tk1, zero, fold(vt, odd), tv1, zero]
        heads.append(jnp.concatenate(rows, axis=0))

    head_tiles((k, v, tk, tv), (gains[0:1], None, gains[1:2], None), add)
    send_copies(out, copies, heads)


def pack_queries(place, q, gains, out):
    zero = jnp.zeros((2, 128), f32)
    heads = []

    def add(tiles, odd):
        heads.append(jnp.concatenate([fold(tiles[0], odd) * 0.125, zero], axis=0))

    head_tiles((q,), (gains[...],), add)
    for g in range(GROUPS):
        message = jnp.concatenate(heads[PER * g : PER * (g + 1)], axis=0).astype(bf16)
        out[jnp.bitwise_xor(place[0], g)] = message


def spread_kernel(*refs):
    *blocks, same, other = refs
    rows = 8 * GROUPS
    for d, block in enumerate(blocks):
        for j in range(PER):
            q = rows_of(block[:, 8 * j : 8 * j + 8, :].astype(f32))
            same[j, rows * d : rows * (d + 1), :] = q.astype(bf16)
            other[j, rows * d : rows * (d + 1), :] = swap(q).astype(bf16)


def rows_of(block):
    return block.reshape(block.shape[0] * block.shape[1], block.shape[2])


def dot_t(a, b):
    return lax.dot_general(a, b, (((1,), (1,)), ((), ())), preferred_element_type=f32)


def attend_kernel(place, same, other, kv_in, out):
    peers_q = same.shape[1] // 8
    peers_k = kv_in.shape[0]
    keys = peers_k * 8
    queries = peers_q * 8
    left_k = left_lanes((keys, 128))
    left_q = left_lanes((queries, 128))
    lane_q = lax.broadcasted_iota(jnp.int32, (queries, 128), 1)
    row_kind = lax.broadcasted_iota(jnp.int32, (1, keys), 1) & 7
    image = row_kind < HALF
    stats = jnp.zeros((queries, 128), f32)
    tiles = []
    for j in range(PER):
        kv = kv_in[:, 16 * j : 16 * j + 16, :].astype(f32)
        k = rows_of(kv[:, 0:8])
        v = rows_of(kv[:, 8:16])
        if j == 0:
            pick = (lax.broadcasted_iota(jnp.int32, (8, 128), 1) == DH).astype(bf16)
            flags = dot_t(pick, k.astype(bf16))[0:1]
            text = (row_kind == HALF) & (flags > 0.5)
            bias_l = jnp.where(image | text, 0.0, masked_score)
            bias_r = jnp.where(image, 0.0, masked_score)
        q_same = same[j]
        q_swap = other[j]
        k_l = jnp.where(left_k, k, 0.0).astype(bf16)
        k_r = jnp.where(left_k, 0.0, k).astype(bf16)
        v_same = v.astype(bf16)
        v_swap = swap(v).astype(bf16)
        sides = []
        for side in range(2):
            s_l = dot_t(q_swap if side else q_same, k_l) + bias_l
            s_r = dot_t(q_same if side else q_swap, k_r) + bias_r
            top = jnp.max(jnp.maximum(s_l, s_r), axis=-1, keepdims=True)
            top = top.astype(bf16).astype(f32)
            p_l = jnp.exp(s_l - top)
            p_r = jnp.exp(s_r - top)
            den = jnp.sum(p_l + p_r, axis=-1, keepdims=True)
            num = jnp.dot(
                p_l.astype(bf16), v_swap if side else v_same, preferred_element_type=f32
            ) + jnp.dot(
                p_r.astype(bf16), v_same if side else v_swap, preferred_element_type=f32
            )
            den_hi = den.astype(bf16).astype(f32)
            lane = 8 * side + j
            stats = jnp.where(lane_q == lane, top, stats)
            stats = jnp.where(lane_q == lane + 16, den_hi, stats)
            stats = jnp.where(lane_q == lane + 32, den - den_hi, stats)
            sides.append(num)
        tiles.append(jnp.where(left_q, sides[0], sides[1]).reshape(peers_q, 8, 128))
    tiles.append(stats.reshape(peers_q, 8, 128))
    for j in range(0, PER + 1, 2):
        pair = jnp.concatenate([tiles[j], tiles[j + 1]], axis=1).astype(bf16)
        for b in range(peers_q):
            owner = jnp.bitwise_xor(place[0], b % GROUPS) * (peers_q // GROUPS)
            owner += jnp.bitwise_xor(place[1], b // GROUPS)
            out[owner, 8 * j : 8 * j + 16, :] = pair[b]


def merge_kernel(parts_in, weight, out):
    blocks = parts_in.shape[0] // GROUPS
    left = left_lanes((blocks, 8, 128))
    left8 = left_lanes((8, 128))
    total = jnp.zeros((16, DH), f32)
    for g in range(GROUPS):
        part = parts_in[g * blocks : (g + 1) * blocks].astype(f32)
        stats = part[:, 8 * PER :, :]
        den = pltpu.roll(stats, 128 - 16, 2) + pltpu.roll(stats, 128 - 32, 2)
        top = jnp.max(stats, axis=0, keepdims=True)
        scale = jnp.exp(stats - top)
        whole = jnp.sum(scale * den, axis=0, keepdims=True)
        share = scale / whole
        for j in range(PER):
            h = PER * g + j
            if h >= HEADS:
                continue
            each = jnp.where(left, share[:, :, j : j + 1], share[:, :, 8 + j : 9 + j])
            attended = jnp.sum(each * part[:, 8 * j : 8 * j + 8, :], axis=0)
            attended = attended.astype(bf16).astype(f32)
            both = jnp.concatenate(
                [jnp.where(left8, attended, 0.0), jnp.where(left8, 0.0, attended)], axis=0
            ).astype(bf16)
            rows = weight[DH * h : DH * (h + 1), :]
            total += jnp.dot(
                both, jnp.concatenate([rows, rows], axis=0), preferred_element_type=f32
            )
    out[...] = total


def on_device(
    img_queries,
    img_keys,
    img_values,
    text_keys,
    text_values,
    query_gain,
    key_gain,
    text_gain,
    text_lengths,
    text_blocks,
    latent,
    base_velocity,
    out_weight,
    timestep,
):
    count_c = lax.axis_size(C)
    count_r = lax.axis_size(R)
    slot = lax.axis_index(SEQ)
    usable = ((slot < text_lengths[0]) & (text_blocks[0, 0] == 1)).astype(jnp.int32)
    vmem = pl.BlockSpec(memory_space=pltpu.VMEM)
    smem = pl.BlockSpec(memory_space=pltpu.SMEM)
    twice = jnp.concatenate([jnp.stack([key_gain, text_gain])] * 2, axis=1)
    query_twice = jnp.concatenate([query_gain, query_gain]).reshape(1, 2 * DH)
    peers_q = GROUPS * count_c
    place = jnp.stack([lax.axis_index(G), lax.axis_index(C)])
    kv_msg = pl.pallas_call(
        lambda *refs: pack_keys(count_r, *refs),
        out_shape=jax.ShapeDtypeStruct((GROUPS * count_r, 16 * PER, 128), bf16),
        in_specs=[vmem] * 5 + [smem],
        name="pack_keys",
    )(img_keys[0], img_values[0], text_keys[0], text_values[0], twice, usable.reshape(1, 1))
    kv_got = lax.all_to_all(kv_msg, G + R, 0, 0, tiled=True)
    q_msg = pl.pallas_call(
        pack_queries,
        out_shape=jax.ShapeDtypeStruct((GROUPS, 8 * PER, 128), bf16),
        in_specs=[smem, vmem, vmem],
        name="pack_queries",
    )(place, img_queries[0], query_twice)
    got = [q_msg[:1]]
    for d in range(1, GROUPS):
        route = [(i, i ^ d) for i in range(GROUPS)]
        got.append(lax.ppermute(q_msg[d : d + 1], G, route))
    block = jnp.concatenate(got, axis=0)
    blocks = [block]
    for d in range(1, count_c):
        route = [(i, i ^ d) for i in range(count_c)]
        blocks.append(lax.ppermute(block, C, route))
    q_same, q_swap = pl.pallas_call(
        spread_kernel,
        out_shape=(jax.ShapeDtypeStruct((PER, 8 * peers_q, 128), bf16),) * 2,
        name="spread",
    )(*blocks)
    parts = pl.pallas_call(
        attend_kernel,
        out_shape=jax.ShapeDtypeStruct((peers_q, 8 * PER + 8, 128), bf16),
        in_specs=[smem, vmem, vmem, vmem],
        name="attend",
    )(place, q_same, q_swap, kv_got)
    parts_got = lax.all_to_all(parts, G + C, 0, 0, tiled=True)
    change = pl.pallas_call(
        merge_kernel, out_shape=jax.ShapeDtypeStruct((16, DH), f32), name="merge"
    )(parts_got, out_weight)
    change = jnp.concatenate([change[:HALF], change[8 : 8 + HALF]], axis=0)
    velocity = base_velocity[0].astype(f32) + change
    guide_half = lax.axis_index("cfg")
    width = latent.shape[1]
    own_part = jnp.where(guide_half == 0, velocity[:, :width], velocity[:, width:])
    sent_part = jnp.where(guide_half == 0, velocity[:, width:], velocity[:, :width])
    partner = lax.ppermute(sent_part, "cfg", [(0, 1), (1, 0)])
    cond_part = jnp.where(guide_half == 0, own_part, partner)
    uncond_part = jnp.where(guide_half == 0, partner, own_part)
    guided = uncond_part + guidance * (cond_part - uncond_part)
    step_now = timestep[0].astype(f32)
    sigma_now = sigma_at(step_now)
    sigma_next = sigma_at(step_now + 1.0)
    next_latent = latent + (sigma_next - sigma_now) * guided
    denoised = latent - sigma_now * guided
    return (next_latent, denoised)


def build(fine):
    return jax.shard_map(
        on_device,
        mesh=fine,
        in_specs=(
            P("cfg", SEQ, None),
            P("cfg", SEQ, None),
            P("cfg", SEQ, None),
            P("cfg", SEQ, None),
            P("cfg", SEQ, None),
            P(),
            P(),
            P(),
            P("cfg"),
            P("cfg", SEQ),
            P(SEQ, "cfg"),
            P("cfg", SEQ, None),
            P(),
            P(),
        ),
        out_specs=(P(SEQ, "cfg"), P(SEQ, "cfg")),
        check_vma=False,
    )


def solution(mesh):
    devices = mesh.devices.reshape(2, 4, 2, 8, 2, 2)
    return build(Mesh(devices, ("cfg",) + SEQ))
```

```python
import jax
import jax.numpy as jnp
from jax import lax
from jax.experimental import pallas as pl
from jax.experimental.pallas import tpu as pltpu
from jax.sharding import Mesh, PartitionSpec as P


STEPS = 28
HEADS = 19
DH = 64
GROUPS = 4
PER = 5
HALF = 6

epsilon = 1e-06
guidance = 3.5
shift_factor = 3.0
masked_score = -1e30

G = ("zl", "core")
R = ("zh",)
C = ("y", "xh")
SEQ = ("y", "xh", "zh", "zl", "core")

f32 = jnp.float32
bf16 = jnp.bfloat16


def sigma_at(position):
    time_left = 1.0 - position / STEPS
    return shift_factor * time_left / (1.0 + (shift_factor - 1.0) * time_left)


def near(x):
    return pltpu.with_memory_space_constraint(x, pltpu.VMEM)


def left_lanes(shape):
    return lax.broadcasted_iota(jnp.int32, shape, len(shape) - 1) < DH


def swap(x):
    return pltpu.roll(x, DH, x.ndim - 1)


def normed(x, gain):
    left = left_lanes(x.shape)
    squares = x * x
    sum_left = jnp.sum(jnp.where(left, squares, 0.0), axis=-1, keepdims=True)
    sum_right = jnp.sum(jnp.where(left, 0.0, squares), axis=-1, keepdims=True)
    root = jnp.where(
        left,
        lax.rsqrt(sum_left / DH + epsilon),
        lax.rsqrt(sum_right / DH + epsilon),
    )
    return (x * root * gain).astype(bf16).astype(f32)


def fold(tile, odd):
    low, high = tile[:HALF], tile[HALF:]
    left = left_lanes(low.shape)
    if odd:
        return jnp.where(left, swap(low), high)
    return jnp.where(left, low, swap(high))


def head_tiles(refs, gains, wanted):
    for p in range((HEADS + 1) // 2):
        wide = 128 if 128 * (p + 1) <= HEADS * DH else DH
        lanes = slice(128 * p, 128 * p + wide)
        tiles = []
        for ref, gain in zip(refs, gains):
            x = ref[:, lanes].astype(f32)
            if wide < 128:
                x = jnp.concatenate([x, jnp.zeros((x.shape[0], 128 - wide), f32)], axis=1)
            tiles.append(x if gain is None else normed(x, gain))
        for odd in range(2):
            wanted(tiles, odd)


def send_copies(out, copies, heads):
    for g in range(GROUPS):
        message = jnp.concatenate(heads[PER * g : PER * (g + 1)], axis=0).astype(bf16)
        for c in range(copies):
            out[g * copies + c] = message


def pack_keys(copies, k, v, tk, tv, gains, flag, out):
    usable = flag[0, 0].astype(f32)
    zero = jnp.zeros((1, 128), f32)
    left = left_lanes((1, 128))
    heads = []

    def add(tiles, odd):
        kt, vt, tkt, tvt = tiles
        tk1 = swap(tkt) if odd else tkt
        tv1 = swap(tvt) if odd else tvt
        tk1 = jnp.where(left, tk1, usable)
        tv1 = jnp.where(left, tv1, 0.0)
        rows = [fold(kt, odd), tk1, zero, fold(vt, odd), tv1, zero]
        heads.append(jnp.concatenate(rows, axis=0))

    head_tiles((k, v, tk, tv), (gains[0:1], None, gains[1:2], None), add)
    send_copies(out, copies, heads)


def pack_queries(q, gains, out):
    zero = jnp.zeros((2, 128), f32)
    heads = []

    def add(tiles, odd):
        heads.append(jnp.concatenate([fold(tiles[0], odd) * 0.125, zero], axis=0))

    head_tiles((q,), (gains[...],), add)
    for g in range(GROUPS):
        message = jnp.concatenate(heads[PER * g : PER * (g + 1)], axis=0).astype(bf16)
        out[g] = message


def spread_kernel(*refs):
    *blocks, same, other = refs
    start = 0
    for block in blocks:
        rows = 8 * block.shape[0]
        for j in range(PER):
            q = rows_of(block[:, 8 * j : 8 * j + 8, :].astype(f32))
            same[j, start : start + rows, :] = q.astype(bf16)
            other[j, start : start + rows, :] = swap(q).astype(bf16)
        start += rows


def rows_of(block):
    return block.reshape(block.shape[0] * block.shape[1], block.shape[2])


def dot_t(a, b):
    return lax.dot_general(a, b, (((1,), (1,)), ((), ())), preferred_element_type=f32)


def attend_kernel(offsets, place, same, other, kv_in, out):
    peers_q = same.shape[1] // 8
    peers_k = kv_in.shape[0]
    keys = peers_k * 8
    queries = peers_q * 8
    left_k = left_lanes((keys, 128))
    left_q = left_lanes((queries, 128))
    lane_q = lax.broadcasted_iota(jnp.int32, (queries, 128), 1)
    row_kind = lax.broadcasted_iota(jnp.int32, (1, keys), 1) & 7
    image = row_kind < HALF
    stats = jnp.zeros((queries, 128), f32)
    tiles = []
    for j in range(PER):
        kv = kv_in[:, 16 * j : 16 * j + 16, :].astype(f32)
        k = rows_of(kv[:, 0:8])
        v = rows_of(kv[:, 8:16])
        if j == 0:
            pick = (lax.broadcasted_iota(jnp.int32, (8, 128), 1) == DH).astype(bf16)
            flags = dot_t(pick, k.astype(bf16))[0:1]
            text = (row_kind == HALF) & (flags > 0.5)
            bias_l = jnp.where(image | text, 0.0, masked_score)
            bias_r = jnp.where(image, 0.0, masked_score)
        q_same = same[j]
        q_swap = other[j]
        k_l = jnp.where(left_k, k, 0.0).astype(bf16)
        k_r = jnp.where(left_k, 0.0, k).astype(bf16)
        v_same = v.astype(bf16)
        v_swap = swap(v).astype(bf16)
        sides = []
        for side in range(2):
            s_l = dot_t(q_swap if side else q_same, k_l) + bias_l
            s_r = dot_t(q_same if side else q_swap, k_r) + bias_r
            top = jnp.max(jnp.maximum(s_l, s_r), axis=-1, keepdims=True)
            top = top.astype(bf16).astype(f32)
            p_l = jnp.exp(s_l - top)
            p_r = jnp.exp(s_r - top)
            den = jnp.sum(p_l + p_r, axis=-1, keepdims=True)
            num = jnp.dot(
                p_l.astype(bf16), v_swap if side else v_same, preferred_element_type=f32
            ) + jnp.dot(
                p_r.astype(bf16), v_same if side else v_swap, preferred_element_type=f32
            )
            den_hi = den.astype(bf16).astype(f32)
            lane = 8 * side + j
            stats = jnp.where(lane_q == lane, top, stats)
            stats = jnp.where(lane_q == lane + 16, den_hi, stats)
            stats = jnp.where(lane_q == lane + 32, den - den_hi, stats)
            sides.append(num)
        tiles.append(jnp.where(left_q, sides[0], sides[1]).reshape(peers_q, 8, 128))
    tiles.append(stats.reshape(peers_q, 8, 128))
    for j in range(0, PER + 1, 2):
        pair = jnp.concatenate([tiles[j], tiles[j + 1]], axis=1).astype(bf16)
        for b in range(peers_q):
            owner = jnp.bitwise_xor(place[0], offsets[b // GROUPS])
            owner += b % GROUPS * len(offsets)
            out[owner, 8 * j : 8 * j + 16, :] = pair[b]


def merge_kernel(half, parts_in, weight, base, own_out, sent_out):
    blocks = parts_in.shape[0] // GROUPS
    left = left_lanes((blocks, 8, 128))
    left8 = left_lanes((8, 128))
    total = jnp.zeros((16, DH), f32)
    for g in range(GROUPS):
        part = parts_in[g * blocks : (g + 1) * blocks].astype(f32)
        stats = part[:, 8 * PER :, :]
        den = pltpu.roll(stats, 128 - 16, 2) + pltpu.roll(stats, 128 - 32, 2)
        top = jnp.max(stats, axis=0, keepdims=True)
        scale = jnp.exp(stats - top)
        whole = jnp.sum(scale * den, axis=0, keepdims=True)
        share = scale / whole
        for j in range(PER):
            h = PER * g + j
            if h >= HEADS:
                continue
            each = jnp.where(left, share[:, :, j : j + 1], share[:, :, 8 + j : 9 + j])
            attended = jnp.sum(each * part[:, 8 * j : 8 * j + 8, :], axis=0)
            attended = attended.astype(bf16).astype(f32)
            both = jnp.concatenate(
                [jnp.where(left8, attended, 0.0), jnp.where(left8, 0.0, attended)], axis=0
            ).astype(bf16)
            rows = weight[DH * h : DH * (h + 1), :]
            total += jnp.dot(
                both, jnp.concatenate([rows, rows], axis=0), preferred_element_type=f32
            )
    change = jnp.concatenate([total[:HALF], total[8 : 8 + HALF]], axis=0)
    velocity = base[...].astype(f32) + change
    low, high = velocity[:, : DH // 2], velocity[:, DH // 2 :]
    own_out[...] = jnp.where(half[0] == 0, low, high)
    sent_out[...] = jnp.where(half[0] == 0, high, low)


def on_device(
    img_queries,
    img_keys,
    img_values,
    text_keys,
    text_values,
    query_gain,
    key_gain,
    text_gain,
    text_lengths,
    text_blocks,
    latent,
    base_velocity,
    out_weight,
    timestep,
):
    count_c = lax.axis_size(C)
    count_r = lax.axis_size(R)
    slot = lax.axis_index(SEQ)
    usable = ((slot < text_lengths[0]) & (text_blocks[0, 0] == 1)).astype(jnp.int32)
    vmem = pl.BlockSpec(memory_space=pltpu.VMEM)
    smem = pl.BlockSpec(memory_space=pltpu.SMEM)
    twice = jnp.concatenate([jnp.stack([key_gain, text_gain])] * 2, axis=1)
    query_twice = jnp.concatenate([query_gain, query_gain]).reshape(1, 2 * DH)
    peers_q = GROUPS * count_c
    place = lax.axis_index(C).reshape(1)
    q_msg = pl.pallas_call(
        pack_queries,
        out_shape=jax.ShapeDtypeStruct((GROUPS, 8 * PER, 128), bf16),
        name="pack_queries",
    )(img_queries[0], query_twice)
    block = lax.all_to_all(q_msg, G, 0, 0, tiled=True)
    kv_msg = pl.pallas_call(
        lambda *refs: pack_keys(count_r, *refs),
        out_shape=jax.ShapeDtypeStruct((GROUPS * count_r, 16 * PER, 128), bf16),
        in_specs=[vmem] * 5 + [smem],
        name="pack_keys",
    )(img_keys[0], img_values[0], text_keys[0], text_values[0], twice, usable.reshape(1, 1))
    kv_got = lax.all_to_all(kv_msg, G + R, 0, 0, tiled=True)
    blocks = [block]
    offsets = [0]
    unit = count_c
    for axis in C:
        size = lax.axis_size(axis)
        unit //= size
        step = 1
        while step < size:
            block = jnp.concatenate(blocks, axis=0) if len(blocks) > 1 else block
            route = [(i, i ^ step) for i in range(size)]
            blocks = [block, lax.ppermute(block, axis, route)]
            offsets += [o ^ (step * unit) for o in offsets]
            step *= 2
    q_same, q_swap = pl.pallas_call(
        spread_kernel,
        out_shape=(jax.ShapeDtypeStruct((PER, 8 * peers_q, 128), bf16),) * 2,
        name="spread",
    )(*[near(block) for block in blocks])
    parts = pl.pallas_call(
        lambda *refs: attend_kernel(offsets, *refs),
        out_shape=jax.ShapeDtypeStruct((peers_q, 8 * PER + 8, 128), bf16),
        in_specs=[smem, vmem, vmem, vmem],
        name="attend",
    )(place, q_same, q_swap, near(kv_got))
    parts_got = lax.all_to_all(parts, G + C, 0, 0, tiled=True)
    guide_half = lax.axis_index("cfg")
    share = jax.ShapeDtypeStruct(latent.shape, f32)
    own_part, sent_part = pl.pallas_call(
        merge_kernel,
        out_shape=(share, share),
        in_specs=[smem, vmem, vmem, vmem],
        name="merge",
    )(guide_half.reshape(1), near(parts_got), out_weight, base_velocity[0])
    partner = lax.ppermute(sent_part, "cfg", [(0, 1), (1, 0)])
    cond_part = jnp.where(guide_half == 0, own_part, partner)
    uncond_part = jnp.where(guide_half == 0, partner, own_part)
    guided = uncond_part + guidance * (cond_part - uncond_part)
    step_now = timestep[0].astype(f32)
    sigma_now = sigma_at(step_now)
    sigma_next = sigma_at(step_now + 1.0)
    next_latent = latent + (sigma_next - sigma_now) * guided
    denoised = latent - sigma_now * guided
    return (next_latent, denoised)


def build(fine):
    return jax.shard_map(
        on_device,
        mesh=fine,
        in_specs=(
            P("cfg", SEQ, None),
            P("cfg", SEQ, None),
            P("cfg", SEQ, None),
            P("cfg", SEQ, None),
            P("cfg", SEQ, None),
            P(),
            P(),
            P(),
            P("cfg"),
            P("cfg", SEQ),
            P(SEQ, "cfg"),
            P("cfg", SEQ, None),
            P(),
            P(),
        ),
        out_specs=(P(SEQ, "cfg"), P(SEQ, "cfg")),
        check_vma=False,
    )


def solution(mesh):
    devices = mesh.devices.reshape(2, 4, 2, 8, 2, 2)
    return build(Mesh(devices, ("cfg",) + SEQ))
```
